32 devices in a mesh: grp: 4 (over y, x), frag: 8 (over z, core).
Axes of the slice: x: 2, y: 2, z: 4, core: 2. Of those that a mesh axis runs over, the one named last changes fastest.
Arguments:
- density: bfloat16 [64, 9216], P('frag'), may hold values from -0.1 to 1, as said below
- fock_blocks: bfloat16 [64, 9216], P('frag'), may hold values from -8 to 8, as said below
- coupling: bfloat16 [128, 9216], P(('grp', 'frag')), may hold values from -1.796875 to 1.796875
- dimer_pairs: int32 [128, 2], P(('grp', 'frag')), may hold values from 0 to 63, as said below
- atom_counts: int32 [64], P('frag'), may hold values from 8 to 16
- nuclear_charge: float32 [1024], P('frag'), may hold values from 4 to 12
- coords: float32 [3, 1024], P(None, 'frag'), may hold values from -120 to 120
Outputs:
- density_correction: float32 [64, 9216], P('frag')
- dimer_energy: float32 [128], P(('grp', 'frag'))
- total_energy: float32 [], replicated
The draws below stay inside these ranges and needn't reach their ends.
Inputs may be any that keep to these rules, and one draw needn't show every extreme that they name: `dimer_pairs`: dimer d has fragments I < J; I // 8 == (d // 4) % 8, and J // 8 lies between I // 8 and I // 8 + 3. `density`: each row is a symmetric matrix. `fock_blocks`: each row is a symmetric matrix.
All inputs are finite; a program needn't handle non-finite values. Where the reference program divides by a largest or mean magnitude, that divisor is 1e-20 or more.
Results may differ from the reference program's by a relative error of at most 0.0018.
Values may be sent and summed in bfloat16 or wider, within the bound.
A program may use at most 64 MiB of HBM per device.

```python
import jax
import jax.numpy as jnp
from jax import lax

NB = 96
NA = 16
REACH = 3
PURIF = 12
FRAG_DEV = 8
DIM_DEV = 4
NFRAG = 64
DIMERS = 128
ATOMS = 1024
N_FRAG = 8


def symmetric_rows(key_main, off_scale, diag_lo, diag_hi):
    key_off, key_diag = jax.random.split(key_main)
    off_noise = off_scale * jax.random.normal(key_off, (NFRAG, NB, NB), jnp.float32)
    occupancy = jax.random.uniform(key_diag, (NFRAG, NB), jnp.float32, diag_lo, diag_hi)
    symmetric = (off_noise + jnp.swapaxes(off_noise, 1, 2)) * 0.7071
    small_eye = jnp.eye(NB, dtype=jnp.float32)[None, :, :]
    blocks = symmetric * (1.0 - small_eye) + occupancy[:, :, None] * small_eye
    return blocks.reshape(NFRAG, NB * NB)


def draw_density(key, part):
    return symmetric_rows(jax.random.fold_in(key, 3), 0.01, 0.15, 0.85).astype(jnp.bfloat16)


def draw_fock_blocks(key, part):
    return symmetric_rows(jax.random.fold_in(key, 5), 0.3, -4.0, 4.0).astype(jnp.bfloat16)


def draw_dimer_pairs(key, part):
    key_first, key_step, key_far = jax.random.split(jax.random.fold_in(key, 11), 3)
    row_index = jnp.arange(DIMERS, dtype=jnp.int32)
    column = row_index // DIM_DEV % N_FRAG
    slot_index = row_index % DIM_DEV
    is_last = (column == N_FRAG - 1).astype(jnp.int32)
    first_local = jax.random.randint(key_first, (DIMERS,), 0, FRAG_DEV - is_last)
    first_frag = column * FRAG_DEV + first_local
    step_size = jax.random.randint(key_step, (DIMERS,), 0, REACH * FRAG_DEV)
    second = jnp.minimum(first_frag + 1 + step_size, NFRAG - 1)
    far_frag = (column + REACH) * FRAG_DEV + jax.random.randint(key_far, (DIMERS,), 0, FRAG_DEV)
    pick_far = jnp.logical_and(slot_index == 0, column + REACH < N_FRAG)
    second = jnp.where(pick_far, far_frag, second)
    return jnp.stack([first_frag, second], axis=1).astype(jnp.int32)


def plant(drawn, key, smallest, top_value):
    longest = drawn.shape.index(max(drawn.shape))
    spots = []
    for shift in (0, 1):
        where = [jax.random.randint(jax.random.fold_in(key, axis), (), 0, length) for axis, length in enumerate(drawn.shape)]
        where[longest] = (where[longest] + shift) % drawn.shape[longest]
        spots.append(tuple(where))
    return drawn.at[spots[0]].set(smallest).at[spots[1]].set(top_value)


def levels(rng, extent, cuts, least, largest):
    level, own = 1.0, jax.random.fold_in(rng, 6)
    for dim, blocks in cuts:
        draws = jnp.exp(jax.random.uniform(jax.random.fold_in(own, dim), (blocks,), jnp.float32, least / len(cuts), largest / len(cuts)))
        level = level * jnp.repeat(draws, extent[dim] // blocks).reshape([-1 if axis == dim else 1 for axis in range(len(extent))])
    return level


def normal_values(rng, shape, scale, bound, cuts=(), kind=jnp.bfloat16):
    entries = scale * jax.random.normal(rng, shape, jnp.float32)
    if cuts:
        entries = entries * levels(rng, shape, cuts, -0.22, 0.18)
    return jnp.clip(entries, -bound, bound).astype(kind)


def setup_inputs(seed: int = 0) -> dict:
    key_list = jax.random.split(jax.random.key(seed), 8)
    return {
        "density": draw_density(jax.random.fold_in(key_list[7], 71), 0),
        "fock_blocks": draw_fock_blocks(jax.random.fold_in(key_list[7], 71), 0),
        "coupling": normal_values(key_list[2], (DIMERS, NB * NB), 0.3, 1.796875, ((0, 32),)),
        "dimer_pairs": draw_dimer_pairs(jax.random.fold_in(key_list[7], 71), 0),
        "atom_counts": plant(jax.random.randint(key_list[4], (NFRAG,), NA // 2, NA + 1), jax.random.fold_in(key_list[4], 1), NA // 2, NA).astype(jnp.int32),
        "nuclear_charge": jnp.clip(4.0 + 8.0 * jax.random.uniform(key_list[5], (ATOMS,), jnp.float32) ** levels(key_list[5], (ATOMS,), ((0, 8),), -0.2, 0.2), 4.0, 12.0),
        "coords": normal_values(key_list[6], (3, ATOMS), 20.0, 120.0, ((1, 8),), jnp.float32),
    }


FULL_PRECISION = lax.Precision.HIGHEST

def basis_atoms(count_real):
    basis_index = jnp.arange(NB, dtype=jnp.float32)[None, :, None]
    atom_index = jnp.arange(NA, dtype=jnp.float32)[None, None, :]
    scaled = basis_index * count_real[:, None, None]
    inside = jnp.logical_and(atom_index * NB <= scaled, scaled < (atom_index + 1.0) * NB)
    return inside.astype(jnp.float32)

def atom_table(density, nuclear_charge, atom_counts, coords):
    frag_count = density.shape[0]
    count_real = atom_counts.astype(jnp.float32)
    owners = basis_atoms(count_real)
    blocks = density.reshape(frag_count, NB, NB).astype(jnp.float32)
    on_diagonal = jnp.diagonal(blocks, axis1=1, axis2=2)
    population = 2.0 * lax.optimization_barrier(jnp.sum(on_diagonal[:, :, None] * owners, axis=1))
    is_live = (jnp.arange(NA, dtype=jnp.float32)[None, :] < count_real[:, None]).astype(jnp.float32)
    charge = is_live * nuclear_charge.reshape(frag_count, NA) - population
    return jnp.concatenate([charge.reshape(1, -1), coords, is_live.reshape(1, -1)], axis=0)

def embed_potential(receivers, pair_ids, atom_rows):
    source_frag = jnp.arange(atom_rows.shape[1], dtype=jnp.int32) // NA
    keep_mask = jnp.logical_and(source_frag != pair_ids[0], source_frag != pair_ids[1]).astype(jnp.float32)
    offsets = receivers[1:4, :, None] - atom_rows[1:4, None, :]
    distance_sq = lax.optimization_barrier(jnp.sum(offsets * offsets, axis=0))
    return lax.optimization_barrier(jnp.sum((keep_mask * atom_rows[0])[None, :] / jnp.sqrt(distance_sq + 1.0), axis=1))

def dimer_solve(dens_pair, fock_pair, coupling_row, potential, count_pair):
    owners = basis_atoms(count_pair)
    site_shift = lax.optimization_barrier(jnp.sum(owners * potential.reshape(2, 1, NA), axis=2))
    dens_blocks = dens_pair.astype(jnp.float32).reshape(2, NB, NB)
    fock_parts = fock_pair.astype(jnp.float32).reshape(2, NB, NB)
    cross_block = coupling_row.astype(jnp.float32).reshape(NB, NB)
    small_eye = jnp.eye(NB, dtype=jnp.float32)
    top_rows = jnp.concatenate([fock_parts[0] + small_eye * site_shift[0][None, :], cross_block], axis=1)
    low_rows = jnp.concatenate([cross_block.T, fock_parts[1] + small_eye * site_shift[1][None, :]], axis=1)
    dimer_fock = jnp.concatenate([top_rows, low_rows], axis=0)
    identity = jnp.eye(2 * NB, dtype=jnp.float32)
    centre = jnp.trace(dimer_fock) / (2.0 * NB)
    shifted = dimer_fock - centre * identity
    width = jnp.max(lax.optimization_barrier(jnp.sum(jnp.abs(shifted), axis=1))) + 1e-06
    start = 0.5 * identity - shifted / (2.0 * width)

    def purify(index, current):
        square = jnp.dot(current, current, precision=FULL_PRECISION)
        return 3.0 * square - 2.0 * jnp.dot(square, current, precision=FULL_PRECISION)
    purified = lax.fori_loop(0, PURIF, purify, start)
    zero_block = jnp.zeros((NB, NB), jnp.float32)
    start_guess = jnp.concatenate([jnp.concatenate([dens_blocks[0], zero_block], axis=1), jnp.concatenate([zero_block, dens_blocks[1]], axis=1)], axis=0)
    energy = jnp.sum((purified - start_guess) * dimer_fock.T)
    changes = jnp.stack([purified[:NB, :NB] - dens_blocks[0], purified[NB:, NB:] - dens_blocks[1]])
    return (changes.reshape(2, NB * NB), energy)

def reference(density, fock_blocks, coupling, dimer_pairs, atom_counts, nuclear_charge, coords):
    atom_rows = atom_table(density, nuclear_charge, atom_counts, coords)

    def solve_one(dimer_item):
        pair_ids, coupling_row = dimer_item
        columns = (pair_ids[:, None] * NA + jnp.arange(NA, dtype=jnp.int32)[None, :]).reshape(-1)
        receivers = jnp.take(atom_rows, columns, axis=1)
        potential = embed_potential(receivers, pair_ids, atom_rows)
        count_pair = lax.optimization_barrier(jnp.sum(receivers[4].reshape(2, NA), axis=1))
        return dimer_solve(jnp.take(density, pair_ids, axis=0), jnp.take(fock_blocks, pair_ids, axis=0), coupling_row, potential, count_pair)
    changes, energies = lax.map(solve_one, (dimer_pairs, coupling))
    flat_blocks = changes.reshape(-1, NB * NB)
    fragment_ids = dimer_pairs.reshape(-1)
    density_correction = jax.ops.segment_sum(flat_blocks, fragment_ids, num_segments=NFRAG)
    return (density_correction, energies, jnp.sum(energies))
```

```python
import functools

import jax
import jax.numpy as jnp
from jax import lax
from jax.experimental import pallas as pl
from jax.experimental.pallas import tpu as pltpu
from jax.sharding import PartitionSpec as P

NB = 96
NA = 16
REACH = 3
PURIF = 12
LANES = 128
F32 = jnp.float32
BF16 = jnp.bfloat16


def iota(shape, dim):
    return lax.broadcasted_iota(jnp.int32, shape, dim)


def split(value):
    high = value.astype(BF16)
    return high, (value - high.astype(F32)).astype(BF16)


def dot(left, right):
    return jnp.dot(left, right, preferred_element_type=F32)


def product3(left, right):
    lh, ll = left
    rh, rl = right
    return dot(lh, rh) + (dot(lh, rl) + dot(ll, rh))


def remote(src, dst, send, recv, axis, index):
    return pltpu.make_async_remote_copy(
        src_ref=src,
        dst_ref=dst,
        send_sem=send,
        recv_sem=recv,
        device_id={axis: index},
        device_id_type=pl.DeviceIdType.MESH,
    )


def kernel(
    nf, ng, pairs, fock, dens, coup, count, nuc, xyz,
    out, eng_out, tot_out,
    tbl, tbl_t, halo, ys, fds, jsend, jrecv, acc, rs_recv, fin, e_all, g_all,
    t_s, t_r, h_s, h_r, j_s, j_r, r_s, r_r, a_s, a_r, e_s, e_r, g_s, g_r,
):
    fd = fock.shape[0]
    nd = coup.shape[0]
    ck = fd // ng
    me = lax.axis_index("frag")
    mg = lax.axis_index("grp")

    barrier = pltpu.get_barrier_semaphore()
    for k in range(1, nf):
        pl.semaphore_signal(barrier, inc=1, device_id={"frag": lax.rem(me + k, nf)}, device_id_type=pl.DeviceIdType.MESH)
    for k in range(1, ng):
        pl.semaphore_signal(barrier, inc=1, device_id={"grp": lax.rem(mg + k, ng)}, device_id_type=pl.DeviceIdType.MESH)

    lane = iota((1, LANES), 1)
    slot = lane & (NA - 1)
    part = lane >> 4
    cnt = count[...]
    scaled = iota((NB, LANES), 0) * cnt
    owned = jnp.logical_and(slot * NB <= scaled, scaled < (slot + 1) * NB)
    eye = iota((NB, NB), 0) == iota((NB, NB), 1)
    gathered = jnp.zeros((NB, LANES), F32)
    own_energy = jnp.zeros((1, LANES), F32)
    for k in range(fd):
        dk = dens[k].astype(F32)
        fk = fock[k].astype(F32)
        diag = jnp.sum(jnp.where(eye, dk, 0.0), axis=1, keepdims=True)
        gathered += jnp.where(jnp.logical_and(owned, part == k), diag, 0.0)
        value = jnp.sum(jnp.sum(dk * fk, axis=0, keepdims=True), axis=1, keepdims=True)
        own_energy = jnp.where(part == k, value, own_energy)
    pop = jnp.sum(gathered, axis=0, keepdims=True)
    ids = jnp.zeros((1, LANES), F32)
    for t in range(nd):
        ids = jnp.where(lane == t, pairs[t, 1].astype(F32), ids)
        ids = jnp.where(lane == nd + t, pairs[t, 0].astype(F32), ids)
    tbl[me, 0:1, :] = jnp.where(slot < cnt, nuc[...], 0.0) - 2.0 * pop
    tbl[me, 1:4, :] = xyz[...]
    tbl[me, 4:5, :] = cnt.astype(F32)
    tbl[me, 5:6, :] = pop
    tbl[me, 6:7, :] = own_energy
    tbl[me, 7:8, :] = ids
    for k in range(fd):
        halo[k] = fock[k]

    pl.semaphore_wait(barrier, nf + ng - 2)

    tcopies = []
    for k in range(1, nf):
        copy = remote(tbl.at[me], tbl.at[me], t_s.at[k], t_r.at[k], "frag", lax.rem(me + k, nf))
        copy.start()
        tcopies.append(copy)
    hcopies = []
    for d in range(1, REACH + 1):
        copy = remote(fock, halo.at[pl.ds(d * fd, fd)], h_s.at[d], h_r.at[d], "frag", lax.rem(me + nf - d, nf))
        hcopies.append(copy)
        pl.when(me >= d)(copy.start)

    for copy in tcopies:
        copy.wait_recv()
    for c in range(nf):
        tbl_t[pl.ds(c * fd, fd)] = jnp.transpose(tbl[c]).reshape(fd, NA, 8)

    source_part = part
    shifts = []
    off_energy = []
    for t in range(nd):
        first, second = pairs[t, 0], pairs[t, 1]
        rows = jnp.concatenate([tbl_t[first], tbl_t[second]], axis=0)
        total = jnp.zeros((2 * NA, LANES), F32)
        for c in range(nf):
            tile = tbl[c]
            ids_here = source_part + c * fd
            keep = jnp.logical_and(ids_here != first, ids_here != second)
            charge = jnp.where(keep, tile[0:1, :], 0.0)
            dx = rows[:, 1:2] - tile[1:2, :]
            dy = rows[:, 2:3] - tile[2:3, :]
            dz = rows[:, 3:4] - tile[3:4, :]
            total += charge * lax.rsqrt(dx * dx + dy * dy + dz * dz + 1.0)
        pot = jnp.sum(total, axis=1, keepdims=True)
        pair_shift = []
        atom = iota((NA, NB), 0)
        basis = iota((NA, NB), 1).astype(F32)
        for h in range(2):
            n_here = rows[h * NA : h * NA + 1, 4:5]
            s = basis * n_here
            low = (atom * NB).astype(F32)
            inside = jnp.logical_and(low <= s, s < low + float(NB))
            pair_shift.append(jnp.sum(jnp.where(inside, pot[h * NA : (h + 1) * NA], 0.0), axis=0, keepdims=True))
        shifts.append(pair_shift)
        off = jnp.sum(pot * rows[:, 5:6], axis=0, keepdims=True)
        off_energy.append(off + rows[0:1, 6:7] + rows[NA : NA + 1, 6:7])

    for d in range(1, REACH + 1):
        pl.when(me + d < nf)(hcopies[d - 1].wait_recv)

    big_eye = iota((2 * NB, 2 * NB), 0) == iota((2 * NB, 2 * NB), 1)
    for t in range(nd):
        first, second = pairs[t, 0], pairs[t, 1]
        fi = halo[jnp.clip(first - me * fd, 0, fd - 1)].astype(F32) + jnp.where(eye, shifts[t][0], 0.0)
        fj = halo[jnp.clip(second - me * fd, 0, (REACH + 1) * fd - 1)].astype(F32) + jnp.where(eye, shifts[t][1], 0.0)
        cross = coup[t].astype(F32)
        full = jnp.concatenate(
            [jnp.concatenate([fi, cross], axis=1), jnp.concatenate([jnp.transpose(cross), fj], axis=1)], axis=0
        )
        fds[t] = full
        trace = jnp.sum(jnp.sum(jnp.where(big_eye, full, 0.0), axis=0, keepdims=True), axis=1, keepdims=True)
        shifted = full - jnp.where(big_eye, trace / (2.0 * NB), 0.0)
        width = jnp.max(jnp.sum(jnp.abs(shifted), axis=0, keepdims=True), axis=1, keepdims=True) + 1e-06
        ys[t] = -shifted / width

    def purify(index, carry):
        for t in range(nd):
            y = ys[t]
            halves = split(y)
            square = product3(halves, halves)
            ys[t] = 1.5 * y - 0.5 * product3(split(square), halves)
        return carry

    lax.fori_loop(0, PURIF, purify, 0)

    energies = jnp.zeros((1, LANES), F32)
    iblocks = []
    jblocks = []
    for t in range(nd):
        y = ys[t]
        full = fds[t]
        trace = jnp.where(big_eye, full, 0.0)
        both = jnp.sum(jnp.sum(trace + y * full, axis=0, keepdims=True), axis=1, keepdims=True)
        energies = jnp.where(lane == t, 0.5 * both - off_energy[t], energies)
        iblocks.append(0.5 * y[:NB, :NB])
        jblock = 0.5 * y[NB:, NB:]
        jblocks.append(jblock)
        jsend[t] = jblock.astype(BF16)
    e_all[me] = jnp.broadcast_to(energies, (8, LANES))
    eng_out[...] = energies

    for k in range(fd):
        base = jnp.where(eye, 0.5, 0.0) - dens[k].astype(F32)
        total = jnp.zeros((NB, NB), F32)
        for t in range(nd):
            here = (me * fd + k).astype(F32)
            total += jnp.where(ids[:, nd + t : nd + t + 1] == here, iblocks[t] + base, 0.0)
            total += jnp.where(ids[:, t : t + 1] == here, jblocks[t] + base, 0.0)
        acc[k] = total

    ecopies = []
    for k in range(1, nf):
        copy = remote(e_all.at[me], e_all.at[me], e_s.at[k], e_r.at[k], "frag", lax.rem(me + k, nf))
        copy.start()
        ecopies.append(copy)
    jcopies = []
    for d in range(1, REACH + 1):
        copy = remote(jsend, jrecv.at[d - 1], j_s.at[d], j_r.at[d], "frag", lax.rem(me + d, nf))
        jcopies.append(copy)
        pl.when(me + d < nf)(copy.start)

    for copy in ecopies:
        copy.wait_recv()
    group_sum = e_all[0]
    for c in range(1, nf):
        group_sum += e_all[c]
    g_all[mg] = group_sum
    for d in range(1, REACH + 1):

        @pl.when(me >= d)
        def _():
            jcopies[d - 1].wait_recv()
            sender = tbl[lax.rem(me + nf - d, nf)]
            for k in range(fd):
                base = jnp.where(eye, 0.5, 0.0) - dens[k].astype(F32)
                total = acc[k]
                for t in range(nd):
                    hit = sender[7:8, t : t + 1] == (me * fd + k).astype(F32)
                    total += jnp.where(hit, jrecv[d - 1, t].astype(F32) + base, 0.0)
                acc[k] = total

    rcopies = []
    for k in range(1, ng):
        peer = lax.rem(mg + k, ng)
        copy = remote(acc.at[pl.ds(peer * ck, ck)], rs_recv.at[k], r_s.at[k], r_r.at[k], "grp", peer)
        copy.start()
        rcopies.append(copy)
        copy = remote(g_all.at[mg], g_all.at[mg], g_s.at[k], g_r.at[k], "grp", peer)
        copy.start()
        rcopies.append(copy)
    for copy in rcopies:
        copy.wait_recv()
    mine = pl.ds(mg * ck, ck)
    total = acc[mine]
    for k in range(1, ng):
        total += rs_recv[k]
    fin[mine] = total
    whole = g_all[0]
    for c in range(1, ng):
        whole += g_all[c]
    tot_out[...] = jnp.sum(whole[0:1, :], axis=1, keepdims=True)
    acopies = []
    for k in range(1, ng):
        copy = remote(fin.at[mine], fin.at[mine], a_s.at[k], a_r.at[k], "grp", lax.rem(mg + k, ng))
        copy.start()
        acopies.append(copy)
    for copy in acopies:
        copy.wait_recv()
    out[...] = fin[...]

    for copy in tcopies + ecopies + rcopies + acopies:
        copy.wait_send()
    for d in range(1, REACH + 1):
        pl.when(me >= d)(hcopies[d - 1].wait_send)
        pl.when(me + d < nf)(jcopies[d - 1].wait_send)


def per_device(nf, ng, density, fock_blocks, coupling, dimer_pairs, atom_counts, nuclear_charge, coords):
    fd = density.shape[0]
    nd = coupling.shape[0]
    ck = fd // ng
    vmem = pl.BlockSpec(memory_space=pltpu.VMEM)
    smem = pl.BlockSpec(memory_space=pltpu.SMEM)
    sem = pltpu.SemaphoreType.DMA
    out, energies, total = pl.pallas_call(
        functools.partial(kernel, nf, ng),
        out_shape=(
            jax.ShapeDtypeStruct((fd, NB, NB), F32),
            jax.ShapeDtypeStruct((1, LANES), F32),
            jax.ShapeDtypeStruct((1, 1), F32),
        ),
        in_specs=[smem] + [vmem] * 6,
        out_specs=(vmem, vmem, vmem),
        scratch_shapes=[
            pltpu.VMEM((nf, 8, LANES), F32),
            pltpu.VMEM((nf * fd, NA, 8), F32),
            pltpu.VMEM(((REACH + 1) * fd, NB, NB), BF16),
            pltpu.VMEM((nd, 2 * NB, 2 * NB), F32),
            pltpu.VMEM((nd, 2 * NB, 2 * NB), F32),
            pltpu.VMEM((nd, NB, NB), BF16),
            pltpu.VMEM((REACH, nd, NB, NB), BF16),
            pltpu.VMEM((fd, NB, NB), F32),
            pltpu.VMEM((ng, ck, NB, NB), F32),
            pltpu.VMEM((fd, NB, NB), F32),
            pltpu.VMEM((nf, 8, LANES), F32),
            pltpu.VMEM((ng, 8, LANES), F32),
        ]
        + [sem((nf,))] * 2
        + [sem((REACH + 1,))] * 4
        + [sem((ng,))] * 4
        + [sem((nf,))] * 2
        + [sem((ng,))] * 2,
        compiler_params=pltpu.CompilerParams(collective_id=0, has_side_effects=True, vmem_limit_bytes=40 << 20),
        name="dimer_step",
    )(
        dimer_pairs,
        fock_blocks.reshape(fd, NB, NB),
        density.reshape(fd, NB, NB),
        coupling.reshape(nd, NB, NB),
        jnp.repeat(atom_counts, NA).reshape(1, LANES),
        nuclear_charge.reshape(1, LANES),
        coords,
    )
    return out.reshape(fd, NB * NB), energies[0, :nd], total[0, 0]


def solution(mesh):
    nf, ng = mesh.shape["frag"], mesh.shape["grp"]
    return jax.shard_map(
        functools.partial(per_device, nf, ng),
        mesh=mesh,
        in_specs=(
            P("frag", None),
            P("frag", None),
            P(("grp", "frag"), None),
            P(("grp", "frag"), None),
            P("frag"),
            P("frag"),
            P(None, "frag"),
        ),
        out_specs=(P("frag", None), P(("grp", "frag")), P()),
        check_vma=False,
    )
```

```python
import functools

import jax
import jax.numpy as jnp
from jax import lax
from jax.experimental import pallas as pl
from jax.experimental.pallas import tpu as pltpu
from jax.sharding import PartitionSpec as P

NB = 96
NA = 16
REACH = 3
PURIF = 12
EARLY = 6
LANES = 128
F32 = jnp.float32
BF16 = jnp.bfloat16


def iota(shape, dim):
    return lax.broadcasted_iota(jnp.int32, shape, dim)


def split(value):
    high = value.astype(BF16)
    return high, (value - high.astype(F32)).astype(BF16)


def dot(left, right):
    return jnp.dot(left, right, preferred_element_type=F32)


def product3(left, right):
    lh, ll = left
    rh, rl = right
    return dot(lh, rh) + (dot(lh, rl) + dot(ll, rh))


def product1(left, right):
    return dot(left.astype(BF16), right.astype(BF16))


def grid():
    return iota((NB, NB), 0), iota((NB, NB), 1)


def pack(first, second):
    row, col = grid()
    diag = jnp.sum(jnp.where(row == col, second, 0.0), axis=1, keepdims=True)
    return jnp.where(row <= col, first, second), jnp.broadcast_to(diag, (NB, LANES - NB))


def unpack_first(main, flipped):
    row, col = grid()
    return jnp.where(row <= col, main, flipped)


def unpack_second(main, flipped, diag):
    row, col = grid()
    return jnp.where(row > col, main, jnp.where(row == col, diag, flipped))


def remote(src, dst, send, recv, axis, index):
    return pltpu.make_async_remote_copy(
        src_ref=src,
        dst_ref=dst,
        send_sem=send,
        recv_sem=recv,
        device_id={axis: index},
        device_id_type=pl.DeviceIdType.MESH,
    )


def kernel(
    nf, ng, pairs, fock, dens, coup, count, nuc, xyz,
    out, eng_out, tot_out,
    tbl, tbl_t, halo, ys, fds, jsend, jrecv, acc, rs_src, rs_recv, fin, e_all, g_all,
    t_s, t_r, h_s, h_r, j_s, j_r, r_s, r_r, a_s, a_r, e_s, e_r, g_s, g_r,
):
    fd = fock.shape[0]
    fh = fd // 2
    nd = coup.shape[0]
    ck = fd // ng
    paired = ck % 2 == 0
    cu = ck // 2 if paired else ck
    me = lax.axis_index("frag")
    mg = lax.axis_index("grp")

    barrier = pltpu.get_barrier_semaphore()
    for k in range(1, nf):
        pl.semaphore_signal(barrier, inc=1, device_id={"frag": lax.rem(me + k, nf)}, device_id_type=pl.DeviceIdType.MESH)
    for k in range(1, ng):
        pl.semaphore_signal(barrier, inc=1, device_id={"grp": lax.rem(mg + k, ng)}, device_id_type=pl.DeviceIdType.MESH)

    lane = iota((1, LANES), 1)
    slot = lane & (NA - 1)
    part = lane >> 4
    cnt = jnp.zeros((1, LANES), jnp.int32)
    for k in range(fd):
        cnt = jnp.where(part == k, count[k], cnt)
    scaled = iota((NB, LANES), 0) * cnt
    owned = jnp.logical_and(slot * NB <= scaled, scaled < (slot + 1) * NB)
    eye = iota((NB, NB), 0) == iota((NB, NB), 1)
    gathered = jnp.zeros((NB, LANES), F32)
    own_energy = jnp.zeros((1, LANES), F32)
    for k in range(fd):
        dk = dens[k].astype(F32)
        fk = fock[k].astype(F32)
        diag = jnp.sum(jnp.where(eye, dk, 0.0), axis=1, keepdims=True)
        gathered += jnp.where(jnp.logical_and(owned, part == k), diag, 0.0)
        value = jnp.sum(jnp.sum(dk * fk, axis=0, keepdims=True), axis=1, keepdims=True)
        own_energy = jnp.where(part == k, value, own_energy)
    pop = jnp.sum(gathered, axis=0, keepdims=True)
    ids = jnp.zeros((1, LANES), F32)
    for t in range(nd):
        ids = jnp.where(lane == t, pairs[1, t].astype(F32), ids)
        ids = jnp.where(lane == nd + t, pairs[0, t].astype(F32), ids)
    tbl[me, 0:1, :] = jnp.where(slot < cnt, nuc[...], 0.0) - 2.0 * pop
    tbl[me, 1:4, :] = xyz[...]
    tbl[me, 4:5, :] = cnt.astype(F32)
    tbl[me, 5:6, :] = pop
    tbl[me, 6:7, :] = own_energy
    tbl[me, 7:8, :] = ids
    for p in range(fh):
        main, diag = pack(fock[2 * p].astype(F32), fock[2 * p + 1].astype(F32))
        halo[p, :, 0:NB] = main.astype(BF16)
        halo[p, :, NB:LANES] = diag.astype(BF16)

    pl.semaphore_wait(barrier, nf + ng - 2)

    tcopies = []
    for k in range(1, nf):
        copy = remote(tbl.at[me], tbl.at[me], t_s.at[k], t_r.at[k], "frag", lax.rem(me + k, nf))
        copy.start()
        tcopies.append(copy)
    hcopies = []
    for d in range(1, REACH + 1):
        copy = remote(halo.at[pl.ds(0, fh)], halo.at[pl.ds(d * fh, fh)], h_s.at[d], h_r.at[d], "frag", lax.rem(me + nf - d, nf))
        hcopies.append(copy)
        pl.when(me >= d)(copy.start)

    for copy in tcopies:
        copy.wait_recv()
    for c in range(nf):
        tbl_t[pl.ds(c * fd, fd)] = jnp.transpose(tbl[c]).reshape(fd, NA, 8)

    source_part = part
    shifts = []
    off_energy = []
    for t in range(nd):
        first, second = pairs[0, t], pairs[1, t]
        rows = jnp.concatenate([tbl_t[first], tbl_t[second]], axis=0)
        total = jnp.zeros((2 * NA, LANES), F32)
        for c in range(nf):
            tile = tbl[c]
            ids_here = source_part + c * fd
            keep = jnp.logical_and(ids_here != first, ids_here != second)
            charge = jnp.where(keep, tile[0:1, :], 0.0)
            dx = rows[:, 1:2] - tile[1:2, :]
            dy = rows[:, 2:3] - tile[2:3, :]
            dz = rows[:, 3:4] - tile[3:4, :]
            total += charge * lax.rsqrt(dx * dx + dy * dy + dz * dz + 1.0)
        pot = jnp.sum(total, axis=1, keepdims=True)
        pair_shift = []
        atom = iota((NA, NB), 0)
        basis = iota((NA, NB), 1).astype(F32)
        for h in range(2):
            n_here = rows[h * NA : h * NA + 1, 4:5]
            s = basis * n_here
            low = (atom * NB).astype(F32)
            inside = jnp.logical_and(low <= s, s < low + float(NB))
            pair_shift.append(jnp.sum(jnp.where(inside, pot[h * NA : (h + 1) * NA], 0.0), axis=0, keepdims=True))
        shifts.append(pair_shift)
        off = jnp.sum(pot * rows[:, 5:6], axis=0, keepdims=True)
        off_energy.append(off + rows[0:1, 6:7] + rows[NA : NA + 1, 6:7])

    for d in range(1, REACH + 1):
        pl.when(me + d < nf)(hcopies[d - 1].wait_recv)

    big_eye = iota((2 * NB, 2 * NB), 0) == iota((2 * NB, 2 * NB), 1)
    for t in range(nd):
        first, second = pairs[0, t], pairs[1, t]
        fi = fock[jnp.clip(first - me * fd, 0, fd - 1)].astype(F32) + jnp.where(eye, shifts[t][0], 0.0)
        where_j = jnp.clip(second - me * fd, 0, (REACH + 1) * fd - 1)
        tile = halo[where_j >> 1].astype(F32)
        main = tile[:, 0:NB]
        flipped = jnp.transpose(main)
        even = ((iota((NB, NB), 0) * 0 + where_j) & 1) == 0
        fj = jnp.where(even, unpack_first(main, flipped), unpack_second(main, flipped, tile[:, NB : NB + 1]))
        fj = fj + jnp.where(eye, shifts[t][1], 0.0)
        cross = coup[t].astype(F32)
        full = jnp.concatenate(
            [jnp.concatenate([fi, cross], axis=1), jnp.concatenate([jnp.transpose(cross), fj], axis=1)], axis=0
        )
        fds[t] = full
        trace = jnp.sum(jnp.sum(jnp.where(big_eye, full, 0.0), axis=0, keepdims=True), axis=1, keepdims=True)
        shifted = full - jnp.where(big_eye, trace / (2.0 * NB), 0.0)
        width = jnp.max(jnp.sum(jnp.abs(shifted), axis=0, keepdims=True), axis=1, keepdims=True) + 1e-06
        ys[t] = -shifted / width

    def purify(index, carry):
        for t in range(nd):
            y = ys[t]
            halves = split(y)
            square = product3(halves, halves)
            ys[t] = 1.5 * y - 0.5 * product3(split(square), halves)
        return carry

    def purify_early(index, carry):
        for t in range(nd):
            y = ys[t]
            ys[t] = 1.5 * y - 0.5 * product1(product1(y, y), y)
        return carry

    lax.fori_loop(0, EARLY, purify_early, 0)
    lax.fori_loop(EARLY, PURIF, purify, 0)

    energies = jnp.zeros((1, LANES), F32)
    for t in range(nd):
        jsend[t] = (0.5 * ys[t, NB:, NB:]).astype(BF16)
    for t in range(nd):
        y = ys[t]
        full = fds[t]
        trace = jnp.where(big_eye, full, 0.0)
        both = jnp.sum(jnp.sum(trace + y * full, axis=0, keepdims=True), axis=1, keepdims=True)
        energies = jnp.where(lane == t, 0.5 * both - off_energy[t], energies)
    e_all[me] = jnp.broadcast_to(energies, (8, LANES))
    eng_out[...] = energies

    jcopies = []
    for d in range(1, REACH + 1):
        copy = remote(jsend, jrecv.at[d - 1], j_s.at[d], j_r.at[d], "frag", lax.rem(me + d, nf))
        jcopies.append(copy)
        pl.when(me + d < nf)(copy.start)

    for k in range(fd):
        base = jnp.where(eye, 0.5, 0.0) - dens[k].astype(F32)
        here = (me * fd + k).astype(F32)
        total = jnp.zeros((NB, NB), F32)
        for t in range(nd):
            total += jnp.where(ids[:, nd + t : nd + t + 1] == here, 0.5 * ys[t, :NB, :NB] + base, 0.0)
            total += jnp.where(ids[:, t : t + 1] == here, 0.5 * ys[t, NB:, NB:] + base, 0.0)
        acc[k] = total

    ecopies = []
    for k in range(1, nf):
        copy = remote(e_all.at[me], e_all.at[me], e_s.at[k], e_r.at[k], "frag", lax.rem(me + k, nf))
        copy.start()
        ecopies.append(copy)

    for copy in ecopies:
        copy.wait_recv()
    group_sum = e_all[0]
    for c in range(1, nf):
        group_sum += e_all[c]
    g_all[mg] = group_sum
    for d in range(1, REACH + 1):

        @pl.when(me >= d)
        def _():
            jcopies[d - 1].wait_recv()
            sender = tbl[lax.rem(me + nf - d, nf)]
            for k in range(fd):
                base = jnp.where(eye, 0.5, 0.0) - dens[k].astype(F32)
                total = acc[k]
                for t in range(nd):
                    hit = sender[7:8, t : t + 1] == (me * fd + k).astype(F32)
                    total += jnp.where(hit, jrecv[d - 1, t].astype(F32) + base, 0.0)
                acc[k] = total

    if paired:
        for p in range(fh):
            main, diag = pack(acc[2 * p], acc[2 * p + 1])
            rs_src[p, :, 0:NB] = main
            rs_src[p, :, NB:LANES] = diag
    else:
        for k in range(fd):
            rs_src[k, :, 0:NB] = acc[k]
    rcopies = []
    for k in range(1, ng):
        peer = lax.rem(mg + k, ng)
        copy = remote(rs_src.at[pl.ds(peer * cu, cu)], rs_recv.at[k], r_s.at[k], r_r.at[k], "grp", peer)
        copy.start()
        rcopies.append(copy)
        copy = remote(g_all.at[mg], g_all.at[mg], g_s.at[k], g_r.at[k], "grp", peer)
        copy.start()
        rcopies.append(copy)
    for copy in rcopies:
        copy.wait_recv()
    mine = pl.ds(mg * cu, cu)
    total = rs_src[mine]
    for k in range(1, ng):
        total += rs_recv[k]
    fin[mine] = total
    whole = g_all[0]
    for c in range(1, ng):
        whole += g_all[c]
    tot_out[...] = jnp.sum(whole[0:1, :], axis=1, keepdims=True)
    acopies = []
    for k in range(1, ng):
        copy = remote(fin.at[mine], fin.at[mine], a_s.at[k], a_r.at[k], "grp", lax.rem(mg + k, ng))
        copy.start()
        acopies.append(copy)
    for copy in acopies:
        copy.wait_recv()
    if paired:
        for p in range(fh):
            tile = fin[p]
            main = tile[:, 0:NB]
            flipped = jnp.transpose(main)
            out[2 * p] = unpack_first(main, flipped)
            out[2 * p + 1] = unpack_second(main, flipped, tile[:, NB : NB + 1])
    else:
        out[...] = fin[:, :, 0:NB]

    for copy in tcopies + ecopies + rcopies + acopies:
        copy.wait_send()
    for d in range(1, REACH + 1):
        pl.when(me >= d)(hcopies[d - 1].wait_send)
        pl.when(me + d < nf)(jcopies[d - 1].wait_send)


def per_device(nf, ng, density, fock_blocks, coupling, dimer_pairs, atom_counts, nuclear_charge, coords):
    fd = density.shape[0]
    nd = coupling.shape[0]
    ck = fd // ng
    cu = ck // 2 if ck % 2 == 0 else ck
    vmem = pl.BlockSpec(memory_space=pltpu.VMEM)
    smem = pl.BlockSpec(memory_space=pltpu.SMEM)
    sem = pltpu.SemaphoreType.DMA
    out, energies, total = pl.pallas_call(
        functools.partial(kernel, nf, ng),
        out_shape=(
            jax.ShapeDtypeStruct((fd, NB, NB), F32),
            jax.ShapeDtypeStruct((1, LANES), F32),
            jax.ShapeDtypeStruct((1, 1), F32),
        ),
        in_specs=[smem] + [vmem] * 3 + [smem] + [vmem] * 2,
        out_specs=(vmem, vmem, vmem),
        scratch_shapes=[
            pltpu.VMEM((nf, 8, LANES), F32),
            pltpu.VMEM((nf * fd, NA, 8), F32),
            pltpu.VMEM(((REACH + 1) * fd // 2, NB, LANES), BF16),
            pltpu.VMEM((nd, 2 * NB, 2 * NB), F32),
            pltpu.VMEM((nd, 2 * NB, 2 * NB), F32),
            pltpu.VMEM((nd, NB, NB), BF16),
            pltpu.VMEM((REACH, nd, NB, NB), BF16),
            pltpu.VMEM((fd, NB, NB), F32),
            pltpu.VMEM((ng * cu, NB, LANES), F32),
            pltpu.VMEM((ng, cu, NB, LANES), F32),
            pltpu.VMEM((ng * cu, NB, LANES), F32),
            pltpu.VMEM((nf, 8, LANES), F32),
            pltpu.VMEM((ng, 8, LANES), F32),
        ]
        + [sem((nf,))] * 2
        + [sem((REACH + 1,))] * 4
        + [sem((ng,))] * 4
        + [sem((nf,))] * 2
        + [sem((ng,))] * 2,
        compiler_params=pltpu.CompilerParams(collective_id=0, has_side_effects=True, vmem_limit_bytes=40 << 20),
        name="dimer_step",
    )(
        dimer_pairs.T,
        fock_blocks.reshape(fd, NB, NB),
        density.reshape(fd, NB, NB),
        coupling.reshape(nd, NB, NB),
        atom_counts,
        nuclear_charge.reshape(1, LANES),
        coords,
    )
    return out.reshape(fd, NB * NB), energies[0, :nd], total[0, 0]


def solution(mesh):
    nf, ng = mesh.shape["frag"], mesh.shape["grp"]
    return jax.shard_map(
        functools.partial(per_device, nf, ng),
        mesh=mesh,
        in_specs=(
            P("frag", None),
            P("frag", None),
            P(("grp", "frag"), None),
            P(("grp", "frag"), None),
            P("frag"),
            P("frag"),
            P(None, "frag"),
        ),
        out_specs=(P("frag", None), P(("grp", "frag")), P()),
        check_vma=False,
    )
```

```python
import functools

import jax
import jax.numpy as jnp
from jax import lax
from jax.experimental import pallas as pl
from jax.experimental.pallas import tpu as pltpu
from jax.sharding import PartitionSpec as P

NB = 96
NA = 16
REACH = 3
PURIF = 12
EARLY = 7
HALVES = 2
LANES = 128
F32 = jnp.float32
BF16 = jnp.bfloat16


def iota(shape, dim):
    return lax.broadcasted_iota(jnp.int32, shape, dim)


def split(value):
    high = value.astype(BF16)
    return high, (value - high.astype(F32)).astype(BF16)


def dot(left, right):
    return jnp.dot(left, right, preferred_element_type=F32)


def product3(left, right):
    lh, ll = left
    rh, rl = right
    return dot(lh, rh) + (dot(lh, rl) + dot(ll, rh))


def product1(left, right):
    return dot(left.astype(BF16), right.astype(BF16))


def grid():
    return iota((NB, NB), 0), iota((NB, NB), 1)


def pack(first, second):
    row, col = grid()
    diag = jnp.sum(jnp.where(row == col, second, 0.0), axis=1, keepdims=True)
    return jnp.where(row <= col, first, second), jnp.broadcast_to(diag, (NB, LANES - NB))


def unpack_first(main, flipped):
    row, col = grid()
    return jnp.where(row <= col, main, flipped)


def unpack_second(main, flipped, diag):
    row, col = grid()
    return jnp.where(row > col, main, jnp.where(row == col, diag, flipped))


def remote(src, dst, send, recv, axis, index):
    return pltpu.make_async_remote_copy(
        src_ref=src,
        dst_ref=dst,
        send_sem=send,
        recv_sem=recv,
        device_id={axis: index},
        device_id_type=pl.DeviceIdType.MESH,
    )


def kernel(
    nf, ng, pairs, fock, dens, coup, count, nuc, xyz,
    out, eng_out, tot_out,
    tbl, tbl_t, halo, ys, fds, jsend, jrecv, acc, rs_src, rs_recv, fin, e_all, g_all,
    t_s, t_r, h_s, h_r, j_s, j_r, r_s, r_r, a_s, a_r, e_s, e_r, g_s, g_r,
):
    fd = fock.shape[0]
    fh = fd // 2
    nd = coup.shape[0]
    ck = fd // ng
    paired = ck % 2 == 0
    cu = ck // 2 if paired else ck
    me = lax.axis_index("frag")
    mg = lax.axis_index("grp")

    barrier = pltpu.get_barrier_semaphore()
    for k in range(1, nf):
        pl.semaphore_signal(barrier, inc=1, device_id={"frag": lax.rem(me + k, nf)}, device_id_type=pl.DeviceIdType.MESH)
    for k in range(1, ng):
        pl.semaphore_signal(barrier, inc=1, device_id={"grp": lax.rem(mg + k, ng)}, device_id_type=pl.DeviceIdType.MESH)

    lane = iota((1, LANES), 1)
    slot = lane & (NA - 1)
    part = lane >> 4
    cnt = jnp.zeros((1, LANES), jnp.int32)
    for k in range(fd):
        cnt = jnp.where(part == k, count[k], cnt)
    scaled = iota((NB, LANES), 0) * cnt
    owned = jnp.logical_and(slot * NB <= scaled, scaled < (slot + 1) * NB)
    eye = iota((NB, NB), 0) == iota((NB, NB), 1)
    gathered = jnp.zeros((NB, LANES), F32)
    own_energy = jnp.zeros((1, LANES), F32)
    for k in range(fd):
        dk = dens[k].astype(F32)
        fk = fock[k].astype(F32)
        diag = jnp.sum(jnp.where(eye, dk, 0.0), axis=1, keepdims=True)
        gathered += jnp.where(jnp.logical_and(owned, part == k), diag, 0.0)
        value = jnp.sum(jnp.sum(dk * fk, axis=0, keepdims=True), axis=1, keepdims=True)
        own_energy = jnp.where(part == k, value, own_energy)
    pop = jnp.sum(gathered, axis=0, keepdims=True)
    ids = jnp.full((1, LANES), -1.0, F32)
    for t in range(nd):
        ids = jnp.where(lane == t, pairs[1, t].astype(F32), ids)
        ids = jnp.where(lane == nd + t, pairs[0, t].astype(F32), ids)
    tbl[me, 0:1, :] = jnp.where(slot < cnt, nuc[...], 0.0) - 2.0 * pop
    tbl[me, 1:4, :] = xyz[...]
    tbl[me, 4:5, :] = cnt.astype(F32)
    tbl[me, 5:6, :] = pop
    tbl[me, 6:7, :] = own_energy
    tbl[me, 7:8, :] = ids
    for p in range(fh):
        main, diag = pack(fock[2 * p].astype(F32), fock[2 * p + 1].astype(F32))
        halo[p, :, 0:NB] = main.astype(BF16)
        halo[p, :, NB:LANES] = diag.astype(BF16)

    pl.semaphore_wait(barrier, nf + ng - 2)

    tcopies = []
    for k in range(1, nf):
        copy = remote(tbl.at[me], tbl.at[me], t_s.at[k], t_r.at[k], "frag", lax.rem(me + k, nf))
        copy.start()
        tcopies.append(copy)
    hcopies = []
    for d in range(1, REACH + 1):
        copy = remote(halo.at[pl.ds(0, fh)], halo.at[pl.ds(d * fh, fh)], h_s.at[d], h_r.at[d], "frag", lax.rem(me + nf - d, nf))
        hcopies.append(copy)
        pl.when(me >= d)(copy.start)

    for t in range(nd):
        cross = coup[t].astype(F32)
        fds[t, 0:NB, 0:NB] = fock[jnp.clip(pairs[0, t] - me * fd, 0, fd - 1)].astype(F32)
        fds[t, 0:NB, NB:] = cross
        fds[t, NB:, 0:NB] = jnp.transpose(cross)

    for copy in tcopies:
        copy.wait_recv()
    for c in range(nf):
        tbl_t[pl.ds(c * fd, fd)] = jnp.transpose(tbl[c]).reshape(fd, NA, 8)

    source_part = part
    shifts = []
    off_energy = []
    for t in range(nd):
        first, second = pairs[0, t], pairs[1, t]
        rows = jnp.concatenate([tbl_t[first], tbl_t[second]], axis=0)
        total = jnp.zeros((2 * NA, LANES), F32)
        for c in range(nf):
            tile = tbl[c]
            ids_here = source_part + c * fd
            keep = jnp.logical_and(ids_here != first, ids_here != second)
            charge = jnp.where(keep, tile[0:1, :], 0.0)
            dx = rows[:, 1:2] - tile[1:2, :]
            dy = rows[:, 2:3] - tile[2:3, :]
            dz = rows[:, 3:4] - tile[3:4, :]
            total += charge * lax.rsqrt(dx * dx + dy * dy + dz * dz + 1.0)
        pot = jnp.sum(total, axis=1, keepdims=True)
        pair_shift = []
        atom = iota((NA, NB), 0)
        basis = iota((NA, NB), 1).astype(F32)
        for h in range(2):
            n_here = rows[h * NA : h * NA + 1, 4:5]
            s = basis * n_here
            low = (atom * NB).astype(F32)
            inside = jnp.logical_and(low <= s, s < low + float(NB))
            pair_shift.append(jnp.sum(jnp.where(inside, pot[h * NA : (h + 1) * NA], 0.0), axis=0, keepdims=True))
        shifts.append(pair_shift)
        off = jnp.sum(pot * rows[:, 5:6], axis=0, keepdims=True)
        off_energy.append(off + rows[0:1, 6:7] + rows[NA : NA + 1, 6:7])

    for d in range(1, REACH + 1):
        pl.when(me + d < nf)(hcopies[d - 1].wait_recv)

    big_eye = iota((2 * NB, 2 * NB), 0) == iota((2 * NB, 2 * NB), 1)
    for t in range(nd):
        where_j = jnp.clip(pairs[1, t] - me * fd, 0, (REACH + 1) * fd - 1)
        tile = halo[where_j >> 1].astype(F32)
        main = tile[:, 0:NB]
        flipped = jnp.transpose(main)
        even = ((iota((NB, NB), 0) * 0 + where_j) & 1) == 0
        fj = jnp.where(even, unpack_first(main, flipped), unpack_second(main, flipped, tile[:, NB : NB + 1]))
        fds[t, NB:, NB:] = fj
        full = fds[t] + jnp.where(big_eye, jnp.concatenate(shifts[t], axis=1), 0.0)
        fds[t] = full
        trace = jnp.sum(jnp.sum(jnp.where(big_eye, full, 0.0), axis=0, keepdims=True), axis=1, keepdims=True)
        shifted = full - jnp.where(big_eye, trace / (2.0 * NB), 0.0)
        width = jnp.max(jnp.sum(jnp.abs(shifted), axis=0, keepdims=True), axis=1, keepdims=True) + 1e-06
        ys[t] = -shifted / width

    def purify(index, carry):
        for t in range(nd):
            y = ys[t]
            halves = split(y)
            square = product3(halves, halves)
            ys[t] = 1.5 * y - 0.5 * product3(split(square), halves)
        return carry

    def purify_early(index, carry):
        for t in range(nd):
            y = ys[t]
            ys[t] = 1.5 * y - 0.5 * product1(product1(y, y), y)
        return carry

    lax.fori_loop(0, EARLY, purify_early, 0)
    lax.fori_loop(EARLY, PURIF, purify, 0)

    energies = jnp.zeros((1, LANES), F32)
    for t in range(nd):
        jsend[t] = (0.5 * ys[t, NB:, NB:]).astype(BF16)
    for t in range(nd):
        y = ys[t]
        full = fds[t]
        trace = jnp.where(big_eye, full, 0.0)
        both = jnp.sum(jnp.sum(trace + y * full, axis=0, keepdims=True), axis=1, keepdims=True)
        energies = jnp.where(lane == t, 0.5 * both - off_energy[t], energies)
    e_all[me] = jnp.broadcast_to(energies, (8, LANES))
    eng_out[...] = energies

    jcopies = []
    for d in range(1, REACH + 1):
        copy = remote(jsend, jrecv.at[d - 1], j_s.at[d], j_r.at[d], "frag", lax.rem(me + d, nf))
        jcopies.append(copy)
        pl.when(me + d < nf)(copy.start)

    for k in range(fd):
        here = (me * fd + k).astype(F32)
        hits = jnp.sum(jnp.where(ids == here, 1.0, 0.0), axis=1, keepdims=True)
        for d in range(1, REACH + 1):
            other = jnp.where(lane < nd, tbl[lax.rem(me + nf - d, nf), 7:8, :], -1.0)
            hits += jnp.sum(jnp.where(jnp.logical_and(other == here, me >= d), 1.0, 0.0), axis=1, keepdims=True)
        total = hits * (jnp.where(eye, 0.5, 0.0) - dens[k].astype(F32))
        for t in range(nd):
            total += jnp.where(ids[:, nd + t : nd + t + 1] == here, 0.5 * ys[t, :NB, :NB], 0.0)
            total += jnp.where(ids[:, t : t + 1] == here, 0.5 * ys[t, NB:, NB:], 0.0)
        acc[k] = total

    ecopies = []
    for k in range(1, nf):
        copy = remote(e_all.at[me], e_all.at[me], e_s.at[k], e_r.at[k], "frag", lax.rem(me + k, nf))
        copy.start()
        ecopies.append(copy)

    for d in range(1, REACH + 1):

        @pl.when(me >= d)
        def _():
            jcopies[d - 1].wait_recv()
            sender = tbl[lax.rem(me + nf - d, nf)]
            for k in range(fd):
                total = acc[k]
                for t in range(nd):
                    hit = sender[7:8, t : t + 1] == (me * fd + k).astype(F32)
                    total += jnp.where(hit, jrecv[d - 1, t].astype(F32), 0.0)
                acc[k] = total

    if paired:
        for p in range(fh):
            main, diag = pack(acc[2 * p], acc[2 * p + 1])
            rs_src[p, :, 0:NB] = main
            rs_src[p, :, NB:LANES] = diag
    else:
        for k in range(fd):
            rs_src[k, :, 0:NB] = acc[k]
    rows_each = NB // HALVES
    mine = pl.ds(mg * cu, cu)
    rcopies = []
    for h in range(HALVES):
        rows = pl.ds(h * rows_each, rows_each)
        for k in range(1, ng):
            peer = lax.rem(mg + k, ng)
            s = h * ng + k
            copy = remote(rs_src.at[pl.ds(peer * cu, cu), rows], rs_recv.at[k, :, rows], r_s.at[s], r_r.at[s], "grp", peer)
            copy.start()
            rcopies.append(copy)
    for copy in ecopies:
        copy.wait_recv()
    group_sum = e_all[0]
    for c in range(1, nf):
        group_sum += e_all[c]
    g_all[mg] = group_sum
    acopies = []
    gcopies = []
    for h in range(HALVES):
        rows = pl.ds(h * rows_each, rows_each)
        for k in range(1, ng):
            rcopies[h * (ng - 1) + k - 1].wait_recv()
        total = rs_src[mine, rows]
        for k in range(1, ng):
            total += rs_recv[k, :, rows]
        fin[mine, rows] = total
        if h == 0:
            for k in range(1, ng):
                copy = remote(g_all.at[mg], g_all.at[mg], g_s.at[k], g_r.at[k], "grp", lax.rem(mg + k, ng))
                copy.start()
                gcopies.append(copy)
        for k in range(1, ng):
            s = h * ng + k
            copy = remote(fin.at[mine, rows], fin.at[mine, rows], a_s.at[s], a_r.at[s], "grp", lax.rem(mg + k, ng))
            copy.start()
            acopies.append(copy)
    for copy in gcopies:
        copy.wait_recv()
    whole = g_all[0]
    for c in range(1, ng):
        whole += g_all[c]
    tot_out[...] = jnp.sum(whole[0:1, :], axis=1, keepdims=True)
    for copy in acopies:
        copy.wait_recv()
    if paired:
        for p in range(fh):
            tile = fin[p]
            main = tile[:, 0:NB]
            flipped = jnp.transpose(main)
            out[2 * p] = unpack_first(main, flipped)
            out[2 * p + 1] = unpack_second(main, flipped, tile[:, NB : NB + 1])
    else:
        out[...] = fin[:, :, 0:NB]

    for copy in tcopies + ecopies + rcopies + gcopies + acopies:
        copy.wait_send()
    for d in range(1, REACH + 1):
        pl.when(me >= d)(hcopies[d - 1].wait_send)
        pl.when(me + d < nf)(jcopies[d - 1].wait_send)


def per_device(nf, ng, density, fock_blocks, coupling, dimer_pairs, atom_counts, nuclear_charge, coords):
    fd = density.shape[0]
    nd = coupling.shape[0]
    ck = fd // ng
    cu = ck // 2 if ck % 2 == 0 else ck
    vmem = pl.BlockSpec(memory_space=pltpu.VMEM)
    smem = pl.BlockSpec(memory_space=pltpu.SMEM)
    sem = pltpu.SemaphoreType.DMA
    out, energies, total = pl.pallas_call(
        functools.partial(kernel, nf, ng),
        out_shape=(
            jax.ShapeDtypeStruct((fd, NB, NB), F32),
            jax.ShapeDtypeStruct((1, LANES), F32),
            jax.ShapeDtypeStruct((1, 1), F32),
        ),
        in_specs=[smem] + [vmem] * 3 + [smem] + [vmem] * 2,
        out_specs=(vmem, vmem, vmem),
        scratch_shapes=[
            pltpu.VMEM((nf, 8, LANES), F32),
            pltpu.VMEM((nf * fd, NA, 8), F32),
            pltpu.VMEM(((REACH + 1) * fd // 2, NB, LANES), BF16),
            pltpu.VMEM((nd, 2 * NB, 2 * NB), F32),
            pltpu.VMEM((nd, 2 * NB, 2 * NB), F32),
            pltpu.VMEM((nd, NB, NB), BF16),
            pltpu.VMEM((REACH, nd, NB, NB), BF16),
            pltpu.VMEM((fd, NB, NB), F32),
            pltpu.VMEM((ng * cu, NB, LANES), F32),
            pltpu.VMEM((ng, cu, NB, LANES), F32),
            pltpu.VMEM((ng * cu, NB, LANES), F32),
            pltpu.VMEM((nf, 8, LANES), F32),
            pltpu.VMEM((ng, 8, LANES), F32),
        ]
        + [sem((nf,))] * 2
        + [sem((REACH + 1,))] * 4
        + [sem((HALVES * ng,))] * 4
        + [sem((nf,))] * 2
        + [sem((ng,))] * 2,
        compiler_params=pltpu.CompilerParams(collective_id=0, has_side_effects=True, vmem_limit_bytes=40 << 20),
        name="dimer_step",
    )(
        dimer_pairs.T,
        fock_blocks.reshape(fd, NB, NB),
        density.reshape(fd, NB, NB),
        coupling.reshape(nd, NB, NB),
        atom_counts,
        nuclear_charge.reshape(1, LANES),
        coords,
    )
    return out.reshape(fd, NB * NB), energies[0, :nd], total[0, 0]


def solution(mesh):
    nf, ng = mesh.shape["frag"], mesh.shape["grp"]
    return jax.shard_map(
        functools.partial(per_device, nf, ng),
        mesh=mesh,
        in_specs=(
            P("frag", None),
            P("frag", None),
            P(("grp", "frag"), None),
            P(("grp", "frag"), None),
            P("frag"),
            P("frag"),
            P(None, "frag"),
        ),
        out_specs=(P("frag", None), P(("grp", "frag")), P()),
        check_vma=False,
    )
```

```python
import functools

import jax
import jax.numpy as jnp
from jax import lax
from jax.experimental import pallas as pl
from jax.experimental.pallas import tpu as pltpu
from jax.sharding import PartitionSpec as P

NB = 96
NA = 16
REACH = 3
PURIF = 12
EARLY = 7
LATE = 1
HALVES = 2
LANES = 128
F32 = jnp.float32
BF16 = jnp.bfloat16


def iota(shape, dim):
    return lax.broadcasted_iota(jnp.int32, shape, dim)


def split(value):
    high = value.astype(BF16)
    return high, (value - high.astype(F32)).astype(BF16)


def dot(left, right):
    return jnp.dot(left, right, preferred_element_type=F32)


def product3(left, right):
    lh, ll = left
    rh, rl = right
    return dot(lh, rh) + (dot(lh, rl) + dot(ll, rh))


def product2(left, right):
    lh, ll = left
    return dot(lh, right) + dot(ll, right)


def product1(left, right):
    return dot(left.astype(BF16), right.astype(BF16))


def grid():
    return iota((NB, NB), 0), iota((NB, NB), 1)


def pack(first, second):
    row, col = grid()
    diag = jnp.sum(jnp.where(row == col, second, 0.0), axis=1, keepdims=True)
    return jnp.where(row <= col, first, second), jnp.broadcast_to(diag, (NB, LANES - NB))


def unpack_first(main, flipped):
    row, col = grid()
    return jnp.where(row <= col, main, flipped)


def unpack_second(main, flipped, diag):
    row, col = grid()
    return jnp.where(row > col, main, jnp.where(row == col, diag, flipped))


def remote(src, dst, send, recv, axis, index):
    return pltpu.make_async_remote_copy(
        src_ref=src,
        dst_ref=dst,
        send_sem=send,
        recv_sem=recv,
        device_id={axis: index},
        device_id_type=pl.DeviceIdType.MESH,
    )


def kernel(
    nf, ng, pairs, fock, dens, coup, count, nuc, xyz,
    out, eng_out, tot_out,
    tbl, tbl_t, halo, ys, fds, jsend, jrecv, acc, rs_src, rs_recv, fin, e_all, g_all,
    t_s, t_r, h_s, h_r, j_s, j_r, r_s, r_r, a_s, a_r, e_s, e_r, g_s, g_r,
):
    fd = fock.shape[0]
    fh = fd // 2
    nd = coup.shape[0]
    ck = fd // ng
    paired = ck % 2 == 0
    cu = ck // 2 if paired else ck
    me = lax.axis_index("frag")
    mg = lax.axis_index("grp")

    barrier = pltpu.get_barrier_semaphore()
    for k in range(1, nf):
        pl.semaphore_signal(barrier, inc=1, device_id={"frag": lax.rem(me + k, nf)}, device_id_type=pl.DeviceIdType.MESH)
    for k in range(1, ng):
        pl.semaphore_signal(barrier, inc=1, device_id={"grp": lax.rem(mg + k, ng)}, device_id_type=pl.DeviceIdType.MESH)

    lane = iota((1, LANES), 1)
    slot = lane & (NA - 1)
    part = lane >> 4
    cnt = jnp.zeros((1, LANES), jnp.int32)
    for k in range(fd):
        cnt = jnp.where(part == k, count[k], cnt)
    scaled = iota((NB, LANES), 0) * cnt
    owned = jnp.logical_and(slot * NB <= scaled, scaled < (slot + 1) * NB)
    eye = iota((NB, NB), 0) == iota((NB, NB), 1)
    gathered = jnp.zeros((NB, LANES), F32)
    own_energy = jnp.zeros((1, LANES), F32)
    for k in range(fd):
        dk = dens[k].astype(F32)
        fk = fock[k].astype(F32)
        diag = jnp.sum(jnp.where(eye, dk, 0.0), axis=1, keepdims=True)
        gathered += jnp.where(jnp.logical_and(owned, part == k), diag, 0.0)
        value = jnp.sum(jnp.sum(dk * fk, axis=0, keepdims=True), axis=1, keepdims=True)
        own_energy = jnp.where(part == k, value, own_energy)
    pop = jnp.sum(gathered, axis=0, keepdims=True)
    ids = jnp.full((1, LANES), -1.0, F32)
    for t in range(nd):
        ids = jnp.where(lane == t, pairs[1, t].astype(F32), ids)
        ids = jnp.where(lane == nd + t, pairs[0, t].astype(F32), ids)
    tbl[me, 0:1, :] = jnp.where(slot < cnt, nuc[...], 0.0) - 2.0 * pop
    tbl[me, 1:4, :] = xyz[...]
    tbl[me, 4:5, :] = cnt.astype(F32)
    tbl[me, 5:6, :] = pop
    tbl[me, 6:7, :] = own_energy
    tbl[me, 7:8, :] = ids
    for p in range(fh):
        main, diag = pack(fock[2 * p].astype(F32), fock[2 * p + 1].astype(F32))
        halo[p, :, 0:NB] = main.astype(BF16)
        halo[p, :, NB:LANES] = diag.astype(BF16)

    pl.semaphore_wait(barrier, nf + ng - 2)

    tcopies = []
    for k in range(1, nf):
        copy = remote(tbl.at[me], tbl.at[me], t_s.at[k], t_r.at[k], "frag", lax.rem(me + k, nf))
        copy.start()
        tcopies.append(copy)
    hcopies = []
    for d in range(1, REACH + 1):
        copy = remote(halo.at[pl.ds(0, fh)], halo.at[pl.ds(d * fh, fh)], h_s.at[d], h_r.at[d], "frag", lax.rem(me + nf - d, nf))
        hcopies.append(copy)
        pl.when(me >= d)(copy.start)

    for t in range(nd):
        cross = coup[t].astype(F32)
        fds[t, 0:NB, 0:NB] = fock[jnp.clip(pairs[0, t] - me * fd, 0, fd - 1)].astype(F32)
        fds[t, 0:NB, NB:] = cross
        fds[t, NB:, 0:NB] = jnp.transpose(cross)

    for copy in tcopies:
        copy.wait_recv()
    for c in range(nf):
        tbl_t[pl.ds(c * fd, fd)] = jnp.transpose(tbl[c]).reshape(fd, NA, 8)

    source_part = part
    shifts = []
    off_energy = []
    for t in range(nd):
        first, second = pairs[0, t], pairs[1, t]
        rows = jnp.concatenate([tbl_t[first], tbl_t[second]], axis=0)
        total = jnp.zeros((2 * NA, LANES), F32)
        for c in range(nf):
            tile = tbl[c]
            ids_here = source_part + c * fd
            keep = jnp.logical_and(ids_here != first, ids_here != second)
            charge = jnp.where(keep, tile[0:1, :], 0.0)
            dx = rows[:, 1:2] - tile[1:2, :]
            dy = rows[:, 2:3] - tile[2:3, :]
            dz = rows[:, 3:4] - tile[3:4, :]
            total += charge * lax.rsqrt(dx * dx + dy * dy + dz * dz + 1.0)
        pot = jnp.sum(total, axis=1, keepdims=True)
        pair_shift = []
        atom = iota((NA, NB), 0)
        basis = iota((NA, NB), 1).astype(F32)
        for h in range(2):
            n_here = rows[h * NA : h * NA + 1, 4:5]
            s = basis * n_here
            low = (atom * NB).astype(F32)
            inside = jnp.logical_and(low <= s, s < low + float(NB))
            pair_shift.append(jnp.sum(jnp.where(inside, pot[h * NA : (h + 1) * NA], 0.0), axis=0, keepdims=True))
        shifts.append(pair_shift)
        off = jnp.sum(pot * rows[:, 5:6], axis=0, keepdims=True)
        off_energy.append(off + rows[0:1, 6:7] + rows[NA : NA + 1, 6:7])

    for d in range(1, REACH + 1):
        pl.when(me + d < nf)(hcopies[d - 1].wait_recv)

    big_eye = iota((2 * NB, 2 * NB), 0) == iota((2 * NB, 2 * NB), 1)
    for t in range(nd):
        where_j = jnp.clip(pairs[1, t] - me * fd, 0, (REACH + 1) * fd - 1)
        tile = halo[where_j >> 1].astype(F32)
        main = tile[:, 0:NB]
        flipped = jnp.transpose(main)
        even = ((iota((NB, NB), 0) * 0 + where_j) & 1) == 0
        fj = jnp.where(even, unpack_first(main, flipped), unpack_second(main, flipped, tile[:, NB : NB + 1]))
        fds[t, NB:, NB:] = fj
        full = fds[t] + jnp.where(big_eye, jnp.concatenate(shifts[t], axis=1), 0.0)
        fds[t] = full
        trace = jnp.sum(jnp.sum(jnp.where(big_eye, full, 0.0), axis=0, keepdims=True), axis=1, keepdims=True)
        shifted = full - jnp.where(big_eye, trace / (2.0 * NB), 0.0)
        width = jnp.max(jnp.sum(jnp.abs(shifted), axis=0, keepdims=True), axis=1, keepdims=True) + 1e-06
        ys[t] = -shifted / width

    def purify(index, carry):
        for t in range(nd):
            y = ys[t]
            halves = split(y)
            square = product3(halves, halves)
            ys[t] = 1.5 * y - 0.5 * product3(split(square), halves)
        return carry

    def purify_early(index, carry):
        for t in range(nd):
            y = ys[t]
            ys[t] = 1.5 * y - 0.5 * product1(product1(y, y), y)
        return carry

    lax.fori_loop(0, EARLY, purify_early, 0)
    def purify_middle(index, carry):
        for t in range(nd):
            y = ys[t]
            halves = split(y)
            square = product2(halves, halves[0])
            ys[t] = 1.5 * y - 0.5 * product2(split(square), halves[0])
        return carry

    lax.fori_loop(EARLY, PURIF - LATE, purify_middle, 0)
    lax.fori_loop(PURIF - LATE, PURIF, purify, 0)

    energies = jnp.zeros((1, LANES), F32)
    for t in range(nd):
        jsend[t] = (0.5 * ys[t, NB:, NB:]).astype(BF16)
    for t in range(nd):
        y = ys[t]
        full = fds[t]
        trace = jnp.where(big_eye, full, 0.0)
        both = jnp.sum(jnp.sum(trace + y * full, axis=0, keepdims=True), axis=1, keepdims=True)
        energies = jnp.where(lane == t, 0.5 * both - off_energy[t], energies)
    e_all[me] = jnp.broadcast_to(energies, (8, LANES))
    eng_out[...] = energies[:, :nd]

    jcopies = []
    for d in range(1, REACH + 1):
        copy = remote(jsend, jrecv.at[d - 1], j_s.at[d], j_r.at[d], "frag", lax.rem(me + d, nf))
        jcopies.append(copy)
        pl.when(me + d < nf)(copy.start)

    for k in range(fd):
        here = (me * fd + k).astype(F32)
        hits = jnp.sum(jnp.where(ids == here, 1.0, 0.0), axis=1, keepdims=True)
        for d in range(1, REACH + 1):
            other = jnp.where(lane < nd, tbl[lax.rem(me + nf - d, nf), 7:8, :], -1.0)
            hits += jnp.sum(jnp.where(jnp.logical_and(other == here, me >= d), 1.0, 0.0), axis=1, keepdims=True)
        total = hits * (jnp.where(eye, 0.5, 0.0) - dens[k].astype(F32))
        for t in range(nd):
            total += jnp.where(ids[:, nd + t : nd + t + 1] == here, 0.5 * ys[t, :NB, :NB], 0.0)
            total += jnp.where(ids[:, t : t + 1] == here, 0.5 * ys[t, NB:, NB:], 0.0)
        acc[k] = total

    ecopies = []
    for k in range(1, nf):
        copy = remote(e_all.at[me], e_all.at[me], e_s.at[k], e_r.at[k], "frag", lax.rem(me + k, nf))
        copy.start()
        ecopies.append(copy)

    for d in range(1, REACH + 1):

        @pl.when(me >= d)
        def _():
            jcopies[d - 1].wait_recv()
            sender = tbl[lax.rem(me + nf - d, nf)]
            for k in range(fd):
                total = acc[k]
                for t in range(nd):
                    hit = sender[7:8, t : t + 1] == (me * fd + k).astype(F32)
                    total += jnp.where(hit, jrecv[d - 1, t].astype(F32), 0.0)
                acc[k] = total

    if paired:
        for p in range(fh):
            main, diag = pack(acc[2 * p], acc[2 * p + 1])
            rs_src[p, :, 0:NB] = main
            rs_src[p, :, NB:LANES] = diag
    else:
        for k in range(fd):
            rs_src[k, :, 0:NB] = acc[k]
    rows_each = NB // HALVES
    mine = pl.ds(mg * cu, cu)
    rcopies = []
    for h in range(HALVES):
        rows = pl.ds(h * rows_each, rows_each)
        for k in range(1, ng):
            peer = lax.rem(mg + k, ng)
            s = h * ng + k
            copy = remote(rs_src.at[pl.ds(peer * cu, cu), rows], rs_recv.at[k, :, rows], r_s.at[s], r_r.at[s], "grp", peer)
            copy.start()
            rcopies.append(copy)
    for copy in ecopies:
        copy.wait_recv()
    group_sum = e_all[0]
    for c in range(1, nf):
        group_sum += e_all[c]
    g_all[mg] = group_sum
    acopies = []
    gcopies = []
    for h in range(HALVES):
        rows = pl.ds(h * rows_each, rows_each)
        for k in range(1, ng):
            rcopies[h * (ng - 1) + k - 1].wait_recv()
        total = rs_src[mine, rows]
        for k in range(1, ng):
            total += rs_recv[k, :, rows]
        fin[mine, rows] = total
        if h == 0:
            for k in range(1, ng):
                copy = remote(g_all.at[mg], g_all.at[mg], g_s.at[k], g_r.at[k], "grp", lax.rem(mg + k, ng))
                copy.start()
                gcopies.append(copy)
        for k in range(1, ng):
            s = h * ng + k
            copy = remote(fin.at[mine, rows], fin.at[mine, rows], a_s.at[s], a_r.at[s], "grp", lax.rem(mg + k, ng))
            copy.start()
            acopies.append(copy)
    for copy in gcopies:
        copy.wait_recv()
    whole = g_all[0]
    for c in range(1, ng):
        whole += g_all[c]
    tot_out[...] = jnp.sum(whole[0:1, :], axis=1, keepdims=True)
    for copy in acopies:
        copy.wait_recv()
    if paired:
        for p in range(fh):
            tile = fin[p]
            main = tile[:, 0:NB]
            flipped = jnp.transpose(main)
            out[2 * p] = unpack_first(main, flipped)
            out[2 * p + 1] = unpack_second(main, flipped, tile[:, NB : NB + 1])
    else:
        out[...] = fin[:, :, 0:NB]

    for copy in tcopies + ecopies + rcopies + gcopies + acopies:
        copy.wait_send()
    for d in range(1, REACH + 1):
        pl.when(me >= d)(hcopies[d - 1].wait_send)
        pl.when(me + d < nf)(jcopies[d - 1].wait_send)


def per_device(nf, ng, density, fock_blocks, coupling, dimer_pairs, atom_counts, nuclear_charge, coords):
    fd = density.shape[0]
    nd = coupling.shape[0]
    ck = fd // ng
    cu = ck // 2 if ck % 2 == 0 else ck
    vmem = pl.BlockSpec(memory_space=pltpu.VMEM)
    smem = pl.BlockSpec(memory_space=pltpu.SMEM)
    sem = pltpu.SemaphoreType.DMA
    out, energies, total = pl.pallas_call(
        functools.partial(kernel, nf, ng),
        out_shape=(
            jax.ShapeDtypeStruct((fd, NB, NB), F32),
            jax.ShapeDtypeStruct((1, nd), F32),
            jax.ShapeDtypeStruct((1, 1), F32),
        ),
        in_specs=[smem] + [vmem] * 3 + [smem] + [vmem] * 2,
        out_specs=(vmem, vmem, vmem),
        scratch_shapes=[
            pltpu.VMEM((nf, 8, LANES), F32),
            pltpu.VMEM((nf * fd, NA, 8), F32),
            pltpu.VMEM(((REACH + 1) * fd // 2, NB, LANES), BF16),
            pltpu.VMEM((nd, 2 * NB, 2 * NB), F32),
            pltpu.VMEM((nd, 2 * NB, 2 * NB), F32),
            pltpu.VMEM((nd, NB, NB), BF16),
            pltpu.VMEM((REACH, nd, NB, NB), BF16),
            pltpu.VMEM((fd, NB, NB), F32),
            pltpu.VMEM((ng * cu, NB, LANES), F32),
            pltpu.VMEM((ng, cu, NB, LANES), F32),
            pltpu.VMEM((ng * cu, NB, LANES), F32),
            pltpu.VMEM((nf, 8, LANES), F32),
            pltpu.VMEM((ng, 8, LANES), F32),
        ]
        + [sem((nf,))] * 2
        + [sem((REACH + 1,))] * 4
        + [sem((HALVES * ng,))] * 4
        + [sem((nf,))] * 2
        + [sem((ng,))] * 2,
        compiler_params=pltpu.CompilerParams(collective_id=0, has_side_effects=True, vmem_limit_bytes=40 << 20),
        name="dimer_step",
    )(
        dimer_pairs.T,
        fock_blocks.reshape(fd, NB, NB),
        density.reshape(fd, NB, NB),
        coupling.reshape(nd, NB, NB),
        atom_counts,
        nuclear_charge.reshape(1, LANES),
        coords,
    )
    return out.reshape(fd, NB * NB), energies.reshape(nd), total.reshape(())


def solution(mesh):
    nf, ng = mesh.shape["frag"], mesh.shape["grp"]
    return jax.shard_map(
        functools.partial(per_device, nf, ng),
        mesh=mesh,
        in_specs=(
            P("frag", None),
            P("frag", None),
            P(("grp", "frag"), None),
            P(("grp", "frag"), None),
            P("frag"),
            P("frag"),
            P(None, "frag"),
        ),
        out_specs=(P("frag", None), P(("grp", "frag")), P()),
        check_vma=False,
    )
```
